32 devices in a mesh: ew: 8 (over z, x), ns: 4 (over y, core).
Axes of the slice: x: 2, y: 2, z: 4, core: 2. Of those that a mesh axis runs over, the one named last changes fastest.
Arguments:
- grid: bfloat16 [8, 2, 1280, 5136], P(None, None, 'ns', 'ew'), may hold values from -6 to 6
- band_rows: int32 [1280], replicated, may hold values from 0 to 1279, each once
- wave_pairs: int32 [4], replicated, may hold values from 0 to 323, as said below
- packer_order: int32 [8], replicated, may hold values from 0 to 7, each once
- field_bits: int32 [4], replicated, may hold values from 10 to 14
- field_power: float32 [4], replicated, may hold values from -0.6 to 0.6
- legendre: float32 [4, 1280, 649], P('ns'), may hold values from -0.15625 to 0.15625
Outputs:
- packed: float32 [8, 4, 2, 649], P('ew', 'ns')
The draws below stay inside these ranges and needn't reach their ends.
Inputs may be any that keep to these rules, and one draw needn't show every extreme that they name: `wave_pairs`: distinct values.
All inputs are finite; a program needn't handle non-finite values.
Results may differ from the reference program's by a relative error of at most 0.0003.
Values sent between devices are 32-bit elements; how exact they have to be, the bound alone decides.
No kernel may reach another device: no remote copies, remote signals or barrier semaphores. Data moves between devices by JAX's collectives and lax.ppermute only.
A program may use at most 128 MiB of HBM per device.

```python
import jax
import jax.numpy as jnp
from jax import lax

NLATH = 1280
TRUNC = 647
FIELDS = 4
FL = 8
LEV = 2
PAIRS = 4
NCOL = 649
PADW = 5136


def draw_wave_pairs(key, part):
    halfway = (TRUNC + 1) // 2
    first_key = jax.random.fold_in(key, 11)
    second_key = jax.random.fold_in(key, 23)
    inner = 1 + jax.random.permutation(first_key, halfway - 2)[:PAIRS - 2]
    values = jnp.concatenate([jnp.array([0, halfway - 1], dtype=jnp.int32), inner.astype(jnp.int32)])
    order = jax.random.permutation(second_key, PAIRS)
    return values[order].astype(jnp.int32)


def plant(values, key, low, largest):
    index_at = [jax.random.randint(jax.random.fold_in(key, axis), (), 0, length) for axis, length in enumerate(values.shape)]
    widest = values.shape.index(max(values.shape))
    neighbour = index_at[:widest] + [(index_at[widest] + 1) % values.shape[widest]] + index_at[widest + 1:]
    return values.at[tuple(index_at)].set(low).at[tuple(neighbour)].set(largest)


def steps_of(key, extent, cuts, least, high):
    gain, own = 1.0, jax.random.fold_in(key, 6)
    for position, parts in cuts:
        steps = jnp.exp(jax.random.uniform(jax.random.fold_in(own, position), (parts,), jnp.float32, least / len(cuts), high / len(cuts)))
        gain = gain * jnp.repeat(steps, extent[position] // parts).reshape([-1 if axis == position else 1 for axis in range(len(extent))])
    return gain


def noise(key, dims, scale, reach, cuts=(), kind=jnp.bfloat16):
    gain = steps_of(key, dims, cuts, -0.22, 0.18) if cuts else 1.0
    entries = jax.random.normal(key, dims, jnp.float32) * scale * gain
    return jnp.minimum(jnp.maximum(entries, -reach), reach).astype(kind)


def setup_inputs(seed: int = 0) -> dict:
    splits = jax.random.split(jax.random.key(seed), 8)
    return {
        "grid": noise(splits[0], (FL, 2, NLATH, PADW), 1.0, 6.0, ((2, 4), (3, 8))),
        "band_rows": jax.random.permutation(splits[1], NLATH).astype(jnp.int32),
        "wave_pairs": draw_wave_pairs(jax.random.fold_in(splits[7], 71), 0),
        "packer_order": jax.random.permutation(splits[3], FL).astype(jnp.int32),
        "field_bits": plant(jax.random.randint(splits[4], (FIELDS,), 10, 15), jax.random.fold_in(splits[4], 1), 10, 14).astype(jnp.int32),
        "field_power": jnp.clip(jax.random.uniform(splits[5], (FIELDS,), jnp.float32, -0.6, 0.6), -0.6, 0.6),
        "legendre": noise(splits[6], (PAIRS, NLATH, NCOL), NLATH ** -0.5, 0.15625, ((0, 4),), jnp.float32),
    }


def cycle_table(lat_ids, first_point, point_count, wave_list, truncation):
    lengths = 20 + 4 * lat_ids
    points = first_point + jnp.arange(point_count, dtype=jnp.int32)
    numbers = jnp.stack([wave_list, truncation - wave_list], 1).reshape(-1)
    product = (numbers[None, None, :] * points[None, :, None]) % lengths[:, None, None]
    length_f = lengths.astype(jnp.float32)[:, None, None]
    angles = product.astype(jnp.float32) * (6.283185307179586 / length_f)
    inside = points[None, :, None] < lengths[:, None, None]
    factor = jnp.where(inside, 1.0 / length_f, jnp.float32(0.0))
    trig_values = jnp.stack([jnp.cos(angles) * factor, -jnp.sin(angles) * factor], -1)
    return trig_values.reshape(lat_ids.shape[0], point_count, -1)


def coefficients(ordered, legendre, wave_list, truncation, powers):
    symmetric = ordered[:, 0] + ordered[:, 1]
    antisym = ordered[:, 0] - ordered[:, 1]
    slots, nlat, width = symmetric.shape
    pcount = width // 4
    stacked = jnp.concatenate([symmetric.reshape(slots, nlat, pcount, 4), antisym.reshape(slots, nlat, pcount, 4)], -1)
    result = jnp.einsum("prc,frpq->fpqc", legendre.astype(jnp.float32), stacked.astype(jnp.float32), precision=lax.Precision.HIGHEST)
    columns = jnp.arange(legendre.shape[2], dtype=jnp.int32)[None, :]
    wavenum = wave_list[:, None]
    first_part = columns <= truncation - wavenum
    shifted = columns - (truncation - wavenum + 1)
    even_parity = jnp.where(first_part, columns % 2 == 0, shifted % 2 == 0)
    halves = []
    for e in (0, 1):
        chosen = jnp.where(first_part, jnp.where(even_parity, result[:, :, e], result[:, :, 4 + e]), jnp.where(even_parity, result[:, :, 2 + e], result[:, :, 6 + e]))
        halves.append(chosen)
    coefficient = jnp.stack(halves, 2)
    degree = jnp.where(first_part, wavenum + columns, columns - 1).astype(jnp.float32)
    logs = jnp.log(degree * (degree + 1.0) + 2.0)
    weight = jnp.exp(powers[:, None, None] * logs[None, :, :])
    return coefficient * weight[:, :, None, :]


def slot_settings(slot_fields, field_bits, field_power, levels):
    field_type = slot_fields // levels
    onehot = field_type[:, None] == jnp.arange(field_bits.shape[0], dtype=jnp.int32)[None, :]
    powers = jnp.sum(jnp.where(onehot, field_power[None, :], jnp.float32(0.0)), -1)
    bit_count = jnp.sum(jnp.where(onehot, field_bits[None, :], 0), -1).astype(jnp.float32)
    return powers, (jnp.exp2(bit_count) - 1.0) / 4096.0


def pack_values(scaled, lowest, highest, spread):
    span = highest - lowest + 1e-6
    return (scaled - lowest[:, None, None, None]) / span[:, None, None, None] * spread[:, None, None, None]


def reference(grid, band_rows, wave_pairs, packer_order, field_bits, field_power, legendre):
    point_slots = grid.shape[3]

    def one_row(row):
        trig_values = cycle_table(band_rows[row][None], jnp.int32(0), point_slots, wave_pairs, TRUNC)[0]
        values = lax.dynamic_index_in_dim(grid, row, 2, keepdims=False).astype(jnp.float32)
        return jnp.einsum("fhk,kc->fhc", values, trig_values, precision=lax.Precision.HIGHEST)

    fourier = lax.map(one_row, jnp.arange(NLATH, dtype=jnp.int32))
    fourier = jnp.transpose(fourier, (1, 2, 0, 3))
    ordered = fourier[packer_order]
    powers, spread = slot_settings(packer_order, field_bits, field_power, LEV)
    scaled = coefficients(ordered, legendre, wave_pairs, TRUNC, powers)
    highest = jnp.max(scaled, axis=(1, 2, 3))
    lowest = jnp.min(scaled, axis=(1, 2, 3))
    return pack_values(scaled, lowest, highest, spread)
```

```python
import functools
import jax
import jax.numpy as jnp
from jax import lax
from jax.experimental import pallas as pl
from jax.experimental.pallas import tpu as pltpu
from jax.sharding import PartitionSpec as P

ROWS = 16
LANES = 128


def sincos_of(product, length):
    quarter = length * 0.25
    turns = jnp.round(product * (1.0 / quarter))
    rest = product - turns * quarter
    y = rest * (6.283185307179586 / length)
    y2 = y * y
    sine = y * (1.0 + y2 * (-0.16666654611 + y2 * (0.0083321608736 + y2 * -0.00019515295891)))
    cosine = 1.0 + y2 * (-0.5 + y2 * (0.041666645683 + y2 * (-0.0013887316255 + y2 * 2.4433157118e-05)))
    quadrant = turns.astype(jnp.int32)
    odd = (quadrant & 1) == 1
    upper = (quadrant & 2) == 2
    c = jnp.where(odd, sine, cosine)
    s = jnp.where(odd, cosine, sine)
    minus_c = odd != upper
    return jnp.where(minus_c, -c, c), jnp.where(upper, s, -s)


def fourier_kernel(sizes, order_ref, band_ref, wave_ref, grid_ref, out_ref, hi_ref, lo_ref, acc_ref):
    slots, pairs, rows, segment, truncation, row_axis, point_axis = sizes
    width = 4 * pairs
    blocks = pl.cdiv(segment, LANES)
    step = pl.program_id(0)
    first_row = lax.axis_index(row_axis) * rows + step * ROWS
    first = lax.axis_index(point_axis) * segment

    sub = lax.broadcasted_iota(jnp.int32, (ROWS, LANES), 0)
    lane = lax.broadcasted_iota(jnp.int32, (ROWS, LANES), 1)
    cycle = jnp.zeros((ROWS, LANES), jnp.int32)
    for r in range(ROWS):
        cycle = jnp.where(sub == r, band_ref[first_row + r], cycle)
    length_i = 20 + 4 * cycle
    length = length_i.astype(jnp.float32)
    points = (first + lane).astype(jnp.float32)

    numbers = []
    for p in range(pairs):
        numbers += [wave_ref[p], truncation - wave_ref[p]]
    number_lane = jnp.zeros((ROWS, LANES), jnp.int32)
    for j, number in enumerate(numbers):
        number_lane = jnp.where(lane == j, number, number_lane)
    hop_c, hop_s = sincos_of((number_lane * LANES).astype(jnp.float32), length)

    for j, number in enumerate(numbers):
        c0, s0 = sincos_of(points * number.astype(jnp.float32), length)
        hc = hop_c[:, j : j + 1]
        hs = hop_s[:, j : j + 1]
        twice = jnp.broadcast_to(hc + hc, (ROWS, LANES))
        for a in range(blocks):
            if a == 0:
                c, s = c0, s0
            elif a == 1:
                c, s = c0 * hc - s0 * hs, c0 * hs + s0 * hc
                cp, sp = c0, s0
            else:
                c, s, cp, sp = twice * c - cp, twice * s - sp, c, s
            for e, v in ((0, c), (1, s)):
                hi = v.astype(jnp.bfloat16)
                lo = (v - hi.astype(jnp.float32)).astype(jnp.bfloat16)
                at = (2 * j + e) * ROWS
                hi_ref[at : at + ROWS, a * LANES : (a + 1) * LANES] = hi
                lo_ref[at : at + ROWS, a * LANES : (a + 1) * LANES] = lo

    inside = []
    for a in range(blocks):
        m = (first + a * LANES + lane) < length_i
        if (a + 1) * LANES > segment:
            m = m & (lane < segment - a * LANES)
        inside.append(m)
    pieces = []
    for s in range(slots):
        which = order_ref[s]
        for h in range(2):
            row = grid_ref[which, h]
            cols = []
            for a in range(blocks):
                n = min(LANES, segment - a * LANES)
                cols.append(row[:, a * LANES : a * LANES + n])
            if segment % LANES:
                cols[-1] = jnp.concatenate([cols[-1], jnp.zeros((ROWS, LANES - segment % LANES), row.dtype)], 1)
            pieces.append(jnp.concatenate([jnp.where(m, v, jnp.zeros_like(v)) for m, v in zip(inside, cols)], 1))
    values = jnp.concatenate(pieces, 0)
    dims = (((1,), (1,)), ((), ()))
    product = lax.dot_general(values, hi_ref[...], dims, preferred_element_type=jnp.float32)
    product += lax.dot_general(values, lo_ref[...], dims, preferred_element_type=jnp.float32)

    inverse = 1.0 / length
    inverse = jnp.concatenate([inverse] * (width * ROWS // LANES), 1)
    wide = (ROWS, width * ROWS)
    own = lax.broadcasted_iota(jnp.int32, wide, 0) == lax.broadcasted_iota(jnp.int32, wide, 1) % ROWS
    pick = jnp.where(own, inverse, 0.0)
    picked = jnp.sum(product.reshape(slots * 2, ROWS, width * ROWS) * pick[None], axis=1)
    acc_ref[step] = picked

    @pl.when(step == pl.num_programs(0) - 1)
    def _():
        steps = rows // ROWS
        for p in range(pairs):
            parts = []
            for q in range(4):
                at = (4 * p + q) * ROWS
                parts += [acc_ref[g, :, at : at + ROWS] for g in range(steps)]
            whole = jnp.concatenate(parts, 1)
            for s in range(slots):
                out_ref[s, p] = whole[2 * s : 2 * s + 2]


def fourier(grid, band_rows, wave_pairs, packer_order, truncation, row_axis, point_axis):
    slots, hemispheres, rows, segment = grid.shape
    pairs = wave_pairs.shape[0]
    sizes = (slots, pairs, rows, segment, truncation, row_axis, point_axis)
    padded = pl.cdiv(segment, LANES) * LANES
    width = 4 * pairs
    return pl.pallas_call(
        functools.partial(fourier_kernel, sizes),
        grid_spec=pltpu.PrefetchScalarGridSpec(
            num_scalar_prefetch=3,
            grid=(rows // ROWS,),
            in_specs=[pl.BlockSpec((slots, hemispheres, ROWS, segment), lambda i, *_: (0, 0, i, 0))],
            out_specs=pl.BlockSpec((slots, pairs, 2, 4 * rows), lambda i, *_: (0, 0, 0, 0)),
            scratch_shapes=[
                pltpu.VMEM((width * ROWS, padded), jnp.bfloat16),
                pltpu.VMEM((width * ROWS, padded), jnp.bfloat16),
                pltpu.VMEM((rows // ROWS, slots * 2, width * ROWS), jnp.float32),
            ],
        ),
        out_shape=jax.ShapeDtypeStruct((slots, pairs, 2, 4 * rows), jnp.float32),
        name="fourier_segment",
    )(packer_order, band_rows, wave_pairs, grid)


def legendre_kernel(sizes, order_ref, bits_ref, power_ref, wave_ref, *refs):
    parts, rows, truncation, levels, slot, row_axis, point_axis, slots_here, pair, pairs_here = sizes
    piece_refs, (upper_ref, lower_ref, scaled_ref, stats_ref, band_ref, values_ref) = refs[:parts], refs[parts:]
    me = lax.axis_index(row_axis)
    for d in range(parts):
        band_ref[lax.rem(me + parts - d, parts)] = piece_refs[d][...]
    for b in range(parts):
        north, south = band_ref[b, 0:1, :], band_ref[b, 1:2, :]
        even, odd = north + south, north - south
        for q in range(4):
            values_ref[q : q + 1, b * rows : (b + 1) * rows] = even[:, q * rows : (q + 1) * rows]
            values_ref[4 + q : 5 + q, b * rows : (b + 1) * rows] = odd[:, q * rows : (q + 1) * rows]
    values = values_ref[...]
    high = values.astype(jnp.bfloat16)
    low = (values - high.astype(jnp.float32)).astype(jnp.bfloat16)
    dims = (((1,), (1,)), ((), ()))
    first = lax.dot_general(
        jnp.concatenate([high, low], 0), upper_ref[...], dims, preferred_element_type=jnp.float32
    )
    second = lax.dot_general(high, lower_ref[...], dims, preferred_element_type=jnp.float32)
    result = first[0:8] + first[8:16] + second

    wave = wave_ref[me * pairs_here + pair]
    columns = lax.broadcasted_iota(jnp.int32, (1, result.shape[1]), 1)
    first_part = columns <= truncation - wave
    shifted = columns - (truncation - wave + 1)
    parity = jnp.where(first_part, columns, shifted) & 1
    even_parity = parity == 0
    chosen = jnp.where(
        first_part,
        jnp.where(even_parity, result[0:2], result[4:6]),
        jnp.where(even_parity, result[2:4], result[6:8]),
    )
    degree = jnp.where(first_part, wave + columns, columns - 1).astype(jnp.float32)
    kind = order_ref[lax.axis_index(point_axis) * slots_here + slot] // levels
    weight = jnp.exp(power_ref[kind] * jnp.log(degree * (degree + 1.0) + 2.0))
    scaled = chosen * weight
    scaled_ref[...] = scaled
    lane = lax.broadcasted_iota(jnp.int32, (1, LANES), 1)
    bits = jnp.full((1, LANES), bits_ref[kind], jnp.int32)
    spread = ((1 << bits).astype(jnp.float32) - 1.0) / 4096.0
    stats_ref[...] = jnp.where(lane == 0, jnp.max(scaled), jnp.where(lane == 1, -jnp.min(scaled), spread))


def legendre_part(pieces, upper, lower, order, bits, power, waves, levels, truncation, slot, pair, counts, axes):
    parts = len(pieces)
    rows = pieces[0].shape[1] // 4
    columns = upper.shape[0]
    sizes = (parts, rows, truncation, levels, slot, *axes, counts[0], pair, counts[1])
    scalar = pl.BlockSpec(memory_space=pltpu.SMEM)
    vector = pl.BlockSpec(memory_space=pltpu.VMEM)
    return pl.pallas_call(
        functools.partial(legendre_kernel, sizes),
        in_specs=[scalar] * 4 + [vector] * (parts + 2),
        out_specs=[vector] * 2,
        scratch_shapes=[
            pltpu.VMEM((parts, 2, 4 * rows), jnp.float32),
            pltpu.VMEM((8, parts * rows), jnp.float32),
        ],
        out_shape=[jax.ShapeDtypeStruct((2, columns), jnp.float32), jax.ShapeDtypeStruct((1, LANES), jnp.float32)],
        name="legendre_pair",
    )(order, bits, power, waves, *pieces, upper, lower)


def rounds(value_of, axis):
    count = lax.axis_size(axis)
    me = lax.axis_index(axis)
    moved = [value_of(me)]
    for d in range(1, count):
        to = lax.rem(me + d, count)
        moved.append(lax.ppermute(value_of(to), axis, [(i, (i + d) % count) for i in range(count)]))
    return moved


def shards(grid, band_rows, wave_pairs, packer_order, field_bits, field_power, legendre):
    total_slots = grid.shape[0]
    rows = grid.shape[2]
    sources = lax.axis_size("ew")
    bands = lax.axis_size("ns")
    fl_dev = total_slots // sources
    pair_dev = legendre.shape[0]
    pairs = wave_pairs.shape[0]
    truncation = legendre.shape[2] - 2
    levels = total_slots // field_bits.shape[0]

    terms = fourier(grid, band_rows, wave_pairs, packer_order, truncation, "ns", "ew")
    arrived = lax.all_to_all(terms, "ew", 0, 0, tiled=True)
    summed = jnp.sum(arrived.reshape(sources, fl_dev, pairs, 2, 4 * rows), axis=0)

    turned = jnp.transpose(legendre, (0, 2, 1))
    upper = lax.reduce_precision(turned, 8, 7)
    lower = (turned - upper).astype(jnp.bfloat16)
    upper = upper.astype(jnp.bfloat16)

    outs = []
    for slot in range(fl_dev):
        for pair in range(pair_dev):
            pieces = rounds(
                lambda to: lax.dynamic_index_in_dim(summed[slot], to * pair_dev + pair, 0, keepdims=False), "ns"
            )
            outs.append(
                legendre_part(
                    pieces, upper[pair], lower[pair], packer_order, field_bits, field_power, wave_pairs,
                    levels, truncation, slot, pair, (fl_dev, pair_dev), ("ns", "ew"),
                )
            )
    packed = []
    for slot in range(fl_dev):
        mine = outs[slot * pair_dev : (slot + 1) * pair_dev]
        stats = mine[0][1]
        for _, other in mine[1:]:
            stats = jnp.maximum(stats, other)
        everyone = rounds(lambda to: stats, "ns")
        for other in everyone[1:]:
            stats = jnp.maximum(stats, other)
        highest, lowest, spread = stats[0, 0], -stats[0, 1], stats[0, 2]
        span = highest - lowest + 1e-06
        packed.append(jnp.stack([(scaled - lowest) / span * spread for scaled, _ in mine]))
    return jnp.stack(packed)


def solution(mesh):
    return jax.shard_map(
        shards,
        mesh=mesh,
        in_specs=(P(None, None, "ns", "ew"), P(), P(), P(), P(), P(), P("ns", None, None)),
        out_specs=P("ew", "ns", None, None),
        check_vma=False,
    )
```
